32 devices in a mesh: groups: 2 (over y), wide: 8 (over z, x), narrow: 2 (over core).
Axes of the slice: x: 2, y: 2, z: 4, core: 2. Of those that a mesh axis runs over, the one named last changes fastest.
Arguments:
- goals: float32 [8192, 1024], P(('groups', 'wide', 'narrow')), parts along dimension 0, may hold values from -32 to 32
- premises: float32 [1024, 1024], P(('groups', 'wide', 'narrow')), parts along dimension 0, may hold values from -24 to 24
- counts: int32 [8192], P(('groups', 'wide')), parts along dimension 0, may hold values from 1 to 16
- positives: int32 [8192, 16], P(('groups', 'wide')), parts along dimension 0, may hold values from -1 to 511, as said below
- cotangent: float32 [8192], P(('groups', 'wide')), parts along dimension 0, may hold values from -6 to 6
Outputs:
- goal_loss: float32 [8192], P(('groups', 'wide')), parts along dimension 0
- grad_goals: float32 [8192, 1024], P(('groups', 'wide', 'narrow')), parts along dimension 0
- grad_premises: float32 [1024, 1024], P(('groups', 'wide', 'narrow')), parts along dimension 0
The draws below stay inside these ranges and needn't reach their ends.
There are 2 independent parts, one for each index of `groups`. The reference program is written for one: setup_inputs(seed, part) draws one part's arguments, and reference() takes and returns one part's arrays. A program takes and returns all parts, laid end to end along the dimension named above; each array names one. Nothing has to cross between parts.
Inputs may be any that keep to these rules, and one draw needn't show every extreme that they name: positives[i, k] is a premise index for k < counts[i] and -1 from there on.
All inputs are finite; a program needn't handle non-finite values.
Results may differ from the reference program's by a relative error of at most 0.012.
The reference program's roundings to bfloat16 on the way (of `dscores`) count: a program that leaves them out, or rounds other values in their place, can miss the bound.
Values may be sent and summed in bfloat16 or wider, within the bound.
A program may use at most 64 MiB of HBM per device.

```python
import math
import jax
import jax.numpy as jnp
from jax import lax

E = 1024
K = 16
G = 4096
P_SIZE = 512


def premise_table(key):
    base = jax.random.fold_in(key, 11)
    k_one, k_two = jax.random.split(base, 2)
    signs = jnp.clip(jax.random.normal(k_one, (P_SIZE, E), jnp.float32), -6.0, 6.0)
    scales = jnp.exp(jax.random.uniform(k_two, (P_SIZE, 1), jnp.float32, jnp.log(0.4), jnp.log(4.0)))
    table = signs * scales
    return table


def draw_premises(key, part):
    table = premise_table(key)
    return table


def draw_goals(key, part):
    k_one, k_two = jax.random.split(jax.random.fold_in(key, 31), 2)
    scales = jnp.exp(jax.random.uniform(k_two, (G, 1), jnp.float32, jnp.log(0.5), jnp.log(5.0)))
    return jnp.clip(jax.random.normal(k_one, (G, E), jnp.float32), -6.0, 6.0) * scales


def positive_table(key):
    keys = jax.random.split(jax.random.fold_in(key, 21), 5)
    spread = jax.random.randint(keys[0], (G,), 0, 2) * jax.random.randint(keys[1], (G,), 0, 2)
    base = spread * jax.random.randint(keys[2], (G,), 1, K) + 1
    fullest = jax.random.randint(keys[3], (), 0, G)
    goal_ids = jnp.arange(G)
    counts = jnp.where(goal_ids == fullest, K, base).astype(jnp.int32)
    lists = jax.random.randint(keys[4], (G, K), 0, P_SIZE)
    slots = jnp.arange(K)[None, :]
    lists = jnp.where(slots < counts[:, None], lists, -1)
    lists = jnp.where((goal_ids[:, None] == fullest) & (slots == 0), P_SIZE - 1, lists)
    return (counts, lists.astype(jnp.int32))


def draw_counts(key, part):
    counts, lists = positive_table(key)
    return counts


def draw_positives(key, part):
    counts, lists = positive_table(key)
    return lists


def level_of(stream_key, extent, cuts, low, top_value):
    def one(position, blocks):
        heights = jax.random.uniform(jax.random.fold_in(jax.random.fold_in(stream_key, 6), position), (blocks,), jnp.float32, low / len(cuts), top_value / len(cuts))
        return jnp.repeat(jnp.exp(heights), extent[position] // blocks).reshape((-1,) + (1,) * (len(extent) - position - 1))

    loudness = one(*cuts[0])
    for cut in cuts[1:]:
        loudness = loudness * one(*cut)
    return loudness


def normal_values(key, shape, scale, most, cuts=(), kind=jnp.bfloat16):
    level = level_of(key, shape, cuts, -0.22, 0.18) if cuts else 1.0
    values = jax.random.normal(key, shape, jnp.float32) * scale * level
    return jnp.minimum(jnp.maximum(values, -most), most).astype(kind)


def setup_inputs(seed: int = 0, part: int = 0) -> dict:
    key_list = jax.random.split(jax.random.key(seed), 6)
    part_splits = jax.random.split(jax.random.fold_in(key_list[5], part), 6)
    return {
        "goals": draw_goals(jax.random.fold_in(jax.random.fold_in(key_list[5], part), 71), part),
        "premises": draw_premises(jax.random.fold_in(jax.random.fold_in(key_list[5], part), 71), part),
        "counts": draw_counts(jax.random.fold_in(jax.random.fold_in(key_list[5], part), 71), part),
        "positives": draw_positives(jax.random.fold_in(jax.random.fold_in(key_list[5], part), 71), part),
        "cotangent": normal_values(part_splits[4], (G,), 1.0, 6.0, ((0, 8),), jnp.float32),
    }


def reference(goals, premises, counts, positives, cotangent):
    goal16 = goals.astype(jnp.bfloat16)
    prem16 = premises.astype(jnp.bfloat16)
    scale = E ** -0.5
    block = math.gcd(G, 512)
    steps_count = G // block
    premise_ids = jnp.arange(P_SIZE, dtype=jnp.int32)
    goal_blocks = goal16.reshape(steps_count, block, E)
    list_blocks = positives.reshape(steps_count, block, K)
    count_blocks = counts.astype(jnp.float32).reshape(steps_count, block)
    cot_blocks = cotangent.reshape(steps_count, block)

    def one_block(acc, items):
        rows, lists, cnt, cot = items
        scores = jnp.dot(rows, prem16.T, preferred_element_type=jnp.float32) * scale
        hits = jnp.sum((lists[:, :, None] == premise_ids[None, None, :]).astype(jnp.float32), axis=1)
        top = jnp.max(scores, axis=1)
        lse = top + jnp.log(jnp.sum(jnp.exp(scores - top[:, None]), axis=1))
        pos = jnp.sum(hits * scores, axis=1)
        loss = lse - pos / cnt
        dscores = (cot[:, None] * (jnp.exp(scores - lse[:, None]) - hits / cnt[:, None]) * scale).astype(jnp.bfloat16)
        grad_rows = jnp.dot(dscores, prem16, preferred_element_type=jnp.float32)
        acc = acc + jnp.dot(dscores.T, rows, preferred_element_type=jnp.float32)
        return acc, (loss, grad_rows)

    start = jnp.zeros((P_SIZE, E), jnp.float32)
    grad_premises, (losses, grad_rows) = lax.scan(one_block, start, (goal_blocks, list_blocks, count_blocks, cot_blocks))
    return losses.reshape(G), grad_rows.reshape(G, E), grad_premises
```

```python
import functools

import jax
import jax.numpy as jnp
from jax import lax
from jax.experimental import pallas as pl
from jax.experimental.pallas import tpu as pltpu
from jax.sharding import PartitionSpec as P

MESH = pl.DeviceIdType.MESH


def kernel(
    n_hi,
    n_lo,
    goals_hbm,
    prem_hbm,
    counts_ref,
    positives_ref,
    cot_ref,
    loss_ref,
    dgoal_hbm,
    dprem_ref,
    goals_in,
    prem_in,
    goals_all,
    prem_all,
    weights,
    scores,
    dscores,
    dgoal,
    dprem,
    lo_out,
    lo_in,
    hi_out,
    hi_in,
    local_sems,
    goal_sems,
    ag_send,
    ag_recv,
    fwd_send,
    fwd_recv,
    lo_send,
    lo_recv,
    hi_send,
    hi_recv,
):
    group = lax.axis_index("groups")
    wide = lax.axis_index("wide")
    narrow = lax.axis_index("narrow")
    n_wide = n_hi * n_lo
    hi = wide // n_lo
    lo = wide % n_lo
    rows, width = prem_in.shape
    own_goals = goals_in.shape[0]
    half = n_wide * rows
    scale = width ** (-0.5)

    def hi_peer(a):
        return ((hi + a) % n_hi) * n_lo + lo

    def lo_peer(b):
        return hi * n_lo + (lo + b) % n_lo

    def at(w, n):
        return (group, w, n)

    barrier = pltpu.get_barrier_semaphore()
    for a in range(1, n_hi):
        pl.semaphore_signal(barrier, inc=1, device_id=at(hi_peer(a), narrow), device_id_type=MESH)
    for b in range(1, n_lo):
        pl.semaphore_signal(barrier, inc=1, device_id=at(lo_peer(b), narrow), device_id_type=MESH)
    pl.semaphore_signal(barrier, inc=1, device_id=at(wide, 1 - narrow), device_id_type=MESH)

    load_prem = pltpu.make_async_copy(prem_hbm, prem_in, local_sems.at[0])
    load_prem.start()
    load_goals = pltpu.make_async_copy(goals_hbm, goals_in, local_sems.at[1])
    load_goals.start()

    def block(owner_wide, part):
        start = pl.multiple_of(part * half + owner_wide * rows, rows)
        return prem_all.at[pl.ds(start, rows), :]

    def source(a, b):
        return ((hi + n_hi - a) % n_hi) * n_lo + (lo + n_lo - b) % n_lo

    def hi_copy(a, owner):
        return pltpu.make_async_remote_copy(
            src_ref=block(owner, 0),
            dst_ref=block(owner, 0),
            send_sem=ag_send.at[a * n_lo],
            recv_sem=ag_recv.at[a * n_lo],
            device_id=at(hi_peer(a), narrow),
            device_id_type=MESH,
        )

    def lo_copy(a, b, owner):
        return pltpu.make_async_remote_copy(
            src_ref=block(owner, 0),
            dst_ref=block(owner, 0),
            send_sem=ag_send.at[a * n_lo + b],
            recv_sem=ag_recv.at[a * n_lo + b],
            device_id=at(lo_peer(b), narrow),
            device_id_type=MESH,
        )

    def forward(a, b, owner):
        return pltpu.make_async_remote_copy(
            src_ref=block(owner, 0),
            dst_ref=block(owner, 1),
            send_sem=fwd_send.at[a * n_lo + b],
            recv_sem=fwd_recv.at[a * n_lo + b],
            device_id=at(wide, 1 - narrow),
            device_id_type=MESH,
        )

    load_prem.wait()
    prem_all[pl.ds(pl.multiple_of(wide * rows, rows), rows), :] = prem_in[...].astype(jnp.bfloat16)
    pl.semaphore_wait(barrier, n_hi - 1 + n_lo - 1 + 1)
    for a in range(n_hi - 1, 0, -1):
        hi_copy(a, wide).start()
    for b in range(1, n_lo):
        lo_copy(0, b, wide).start()
    forward(0, 0, wide).start()

    load_goals.wait()
    own_rows = pl.ds(pl.multiple_of(narrow * own_goals, own_goals), own_goals)
    goals_all[own_rows, :] = goals_in[...].astype(jnp.bfloat16)
    goal_copy = pltpu.make_async_remote_copy(
        src_ref=goals_all.at[own_rows, :],
        dst_ref=goals_all.at[own_rows, :],
        send_sem=goal_sems.at[0],
        recv_sem=goal_sems.at[1],
        device_id=at(wide, 1 - narrow),
        device_id_type=MESH,
    )
    goal_copy.start()

    all_goals = goals_all.shape[0]
    lists = positives_ref[...]
    inverse = 1.0 / counts_ref[...].astype(jnp.float32)
    step = 64

    def weigh(number, carry):
        begin = pl.multiple_of(number * step, step)
        local = begin + lax.broadcasted_iota(jnp.int32, (step, all_goals), 0)
        part = local // half
        inner = local - part * half
        owner = inner // rows
        side = narrow + part * (1 - 2 * narrow)
        ids = (owner * 2 + side) * rows + inner % rows
        total = jnp.zeros((step, all_goals), jnp.float32)
        for slot in range(lists.shape[0]):
            total = total + jnp.where(lists[slot : slot + 1, :] == ids, 1.0, 0.0)
        weights[pl.ds(begin, step), :] = total * inverse
        return carry

    lax.fori_loop(0, 2 * half // step, weigh, 0)

    for a in range(1, n_hi):
        owner = source(a, 0)
        hi_copy(a, owner).wait_recv()
        for b in range(1, n_lo):
            lo_copy(a, b, owner).start()
        forward(a, 0, owner).start()
    for a in range(n_hi):
        for b in range(1, n_lo):
            owner = source(a, b)
            lo_copy(a, b, owner).wait_recv()
            forward(a, b, owner).start()
    goal_copy.wait()

    tall = min(256, half)

    def score(begin):
        span = pl.ds(pl.multiple_of(begin, tall), tall)
        scores[span, :] = (
            lax.dot_general(
                prem_all[span, :],
                goals_all[...],
                (((1,), (1,)), ((), ())),
                preferred_element_type=jnp.float32,
            )
            * scale
        )

    pl.loop(0, half // tall)(lambda number: score(number * tall))
    for a in range(n_hi):
        for b in range(n_lo):
            forward(a, b, source(a, b)).wait_recv()
    pl.loop(0, half // tall)(lambda number: score(half + number * tall))

    lanes = 128

    def soften(number, carry):
        cols = pl.ds(pl.multiple_of(number * lanes, lanes), lanes)
        tile = scores[:, cols]
        weight = weights[:, cols]
        top = jnp.max(tile, axis=0, keepdims=True)
        powers = jnp.exp(tile - top)
        total = jnp.sum(powers, axis=0, keepdims=True)
        positive = jnp.sum(weight * tile, axis=0, keepdims=True)
        loss_ref[:, cols] = top + jnp.log(total) - positive
        factor = cot_ref[:, cols] * scale
        dscores[:, cols] = (factor * (powers * (1.0 / total) - weight)).astype(jnp.bfloat16)
        return carry

    lax.fori_loop(0, all_goals // lanes, soften, 0)

    def premise_gradient(number):
        span = pl.ds(pl.multiple_of(number * tall, tall), tall)
        piece = jnp.dot(dscores[span, :], goals_all[...], preferred_element_type=jnp.float32)
        dprem[span, :] = piece
        lo_out[span, :] = piece.astype(jnp.bfloat16)

    pl.loop(0, half // tall)(premise_gradient)

    def lo_reduce(a, b):
        target_hi = (hi + a) % n_hi
        target = target_hi * n_lo + (lo + b) % n_lo
        return pltpu.make_async_remote_copy(
            src_ref=lo_out.at[pl.ds(pl.multiple_of(target * rows, rows), rows), :],
            dst_ref=lo_in.at[a * n_lo + b],
            send_sem=lo_send.at[a * n_lo + b],
            recv_sem=lo_recv.at[a * n_lo + b],
            device_id=at(lo_peer(b), narrow),
            device_id_type=MESH,
        )

    def hi_reduce(a):
        return pltpu.make_async_remote_copy(
            src_ref=hi_out.at[a],
            dst_ref=hi_in.at[a],
            send_sem=hi_send.at[a],
            recv_sem=hi_recv.at[a],
            device_id=at(hi_peer(a), narrow),
            device_id_type=MESH,
        )

    order = list(range(1, n_hi)) + [0]
    for a in order:
        for b in range(1, n_lo):
            lo_reduce(a, b).start()

    def pair_sum(a):
        target = hi_peer(a)
        total = dprem[pl.ds(pl.multiple_of(target * rows, rows), rows), :]
        for b in range(1, n_lo):
            lo_reduce(a, b).wait_recv()
            total = total + lo_in[a * n_lo + b].astype(jnp.float32)
        return total

    if n_lo == 1:
        for a in range(1, n_hi):
            hi_out[a] = pair_sum(a).astype(jnp.bfloat16)
            hi_reduce(a).start()

    dgoal[...] = lax.dot_general(
        dscores[:, pl.ds(pl.multiple_of(narrow * own_goals, own_goals), own_goals)],
        prem_all[...],
        (((0,), (0,)), ((), ())),
        preferred_element_type=jnp.float32,
    )
    store_goals = pltpu.make_async_copy(dgoal, dgoal_hbm, local_sems.at[2])
    store_goals.start()

    if n_lo > 1:
        for a in range(1, n_hi):
            hi_out[a] = pair_sum(a).astype(jnp.bfloat16)
            hi_reduce(a).start()
    mine = pair_sum(0)
    for a in range(1, n_hi):
        hi_reduce(a).wait_recv()
        mine = mine + hi_in[a].astype(jnp.float32)
    dprem_ref[...] = mine

    for a in range(1, n_hi):
        hi_copy(a, wide).wait_send()
        hi_reduce(a).wait_send()
    for a in range(n_hi):
        for b in range(1, n_lo):
            lo_copy(a, b, source(a, 0)).wait_send()
            lo_reduce(a, b).wait_send()
        for b in range(n_lo):
            forward(a, b, source(a, b)).wait_send()
    store_goals.wait()


def per_device(n_wide, goals, premises, counts, positives, cotangent):
    n_lo = 2 if n_wide % 2 == 0 else 1
    n_hi = n_wide // n_lo
    own_goals, width = goals.shape
    rows = premises.shape[0]
    all_goals = counts.shape[0]
    half = n_wide * rows
    bf16, f32 = jnp.bfloat16, jnp.float32
    vmem = pl.BlockSpec(memory_space=pltpu.VMEM)
    anywhere = pl.BlockSpec(memory_space=pl.ANY)
    dma = pltpu.SemaphoreType.DMA
    scratch = [
        pltpu.VMEM((own_goals, width), f32),
        pltpu.VMEM((rows, width), f32),
        pltpu.VMEM((all_goals, width), bf16),
        pltpu.VMEM((2 * half, width), bf16),
        pltpu.VMEM((2 * half, all_goals), f32),
        pltpu.VMEM((2 * half, all_goals), f32),
        pltpu.VMEM((2 * half, all_goals), bf16),
        pltpu.VMEM((own_goals, width), f32),
        pltpu.VMEM((half, width), f32),
        pltpu.VMEM((half, width), bf16),
        pltpu.VMEM((n_wide, rows, width), bf16),
        pltpu.VMEM((n_hi, rows, width), bf16),
        pltpu.VMEM((n_hi, rows, width), bf16),
        dma((3,)),
        dma((2,)),
        dma((n_wide,)),
        dma((n_wide,)),
        dma((n_wide,)),
        dma((n_wide,)),
        dma((n_wide,)),
        dma((n_wide,)),
        dma((n_hi,)),
        dma((n_hi,)),
    ]
    loss, dgoal, dprem = pl.pallas_call(
        functools.partial(kernel, n_hi, n_lo),
        out_shape=(
            jax.ShapeDtypeStruct((1, all_goals), f32),
            jax.ShapeDtypeStruct((own_goals, width), f32),
            jax.ShapeDtypeStruct((rows, width), f32),
        ),
        in_specs=[anywhere, anywhere, vmem, vmem, vmem],
        out_specs=(vmem, anywhere, vmem),
        scratch_shapes=scratch,
        compiler_params=pltpu.CompilerParams(
            collective_id=0, has_side_effects=True, vmem_limit_bytes=58 * 1024 * 1024
        ),
    )(goals, premises, counts.reshape(1, all_goals), positives.T, cotangent.reshape(1, all_goals))
    return (loss.reshape(all_goals), dgoal, dprem)


def solution(mesh):
    return jax.shard_map(
        functools.partial(per_device, mesh.shape["wide"]),
        mesh=mesh,
        in_specs=(
            P(("groups", "wide", "narrow"), None),
            P(("groups", "wide", "narrow"), None),
            P(("groups", "wide")),
            P(("groups", "wide"), None),
            P(("groups", "wide")),
        ),
        out_specs=(
            P(("groups", "wide")),
            P(("groups", "wide", "narrow"), None),
            P(("groups", "wide", "narrow"), None),
        ),
        check_vma=False,
    )
```

```python
import functools

import jax
import jax.numpy as jnp
from jax import lax
from jax.experimental import pallas as pl
from jax.experimental.pallas import tpu as pltpu
from jax.sharding import PartitionSpec as P

MESH = pl.DeviceIdType.MESH


def kernel(
    n_hi,
    n_lo,
    goals_hbm,
    prem_hbm,
    counts_hbm,
    positives_hbm,
    cot_hbm,
    loss_ref,
    dgoal,
    dprem_ref,
    goals_in,
    prem_in,
    counts_ref,
    positives_ref,
    cot_ref,
    goals_all,
    prem_all,
    weights,
    scores,
    dscores,
    dprem,
    lo_out,
    lo_in,
    hi_out,
    hi_in,
    local_sems,
    goal_sems,
    ag_send,
    ag_recv,
    fwd_send,
    fwd_recv,
    lo_send,
    lo_recv,
    hi_send,
    hi_recv,
):
    group = lax.axis_index("groups")
    wide = lax.axis_index("wide")
    narrow = lax.axis_index("narrow")
    n_wide = n_hi * n_lo
    hi = wide // n_lo
    lo = wide % n_lo
    rows, width = prem_in.shape
    own_goals = goals_in.shape[0]
    half = n_wide * rows
    scale = width ** (-0.5)

    def hi_peer(a):
        return ((hi + a) % n_hi) * n_lo + lo

    def lo_peer(b):
        return hi * n_lo + (lo + b) % n_lo

    odd = hi % 2
    if n_hi == 4:
        near_first = [1 + 2 * odd, 3 - 2 * odd, 2]
        arrive_first = [3 - 2 * odd, 1 + 2 * odd, 2]
        far_first = [2, 3 - 2 * odd, 1 + 2 * odd]
    else:
        near_first = arrive_first = far_first = list(range(1, n_hi))

    def at(w, n):
        return (group, w, n)

    barrier = pltpu.get_barrier_semaphore()
    for a in range(1, n_hi):
        pl.semaphore_signal(barrier, inc=1, device_id=at(hi_peer(a), narrow), device_id_type=MESH)
    for b in range(1, n_lo):
        pl.semaphore_signal(barrier, inc=1, device_id=at(lo_peer(b), narrow), device_id_type=MESH)
    pl.semaphore_signal(barrier, inc=1, device_id=at(wide, 1 - narrow), device_id_type=MESH)

    load_prem = pltpu.make_async_copy(prem_hbm, prem_in, local_sems.at[0])
    load_prem.start()
    load_goals = pltpu.make_async_copy(goals_hbm, goals_in, local_sems.at[1])
    load_goals.start()
    small = [(counts_hbm, counts_ref), (positives_hbm, positives_ref), (cot_hbm, cot_ref)]
    small_loads = [
        pltpu.make_async_copy(src, dst, local_sems.at[2 + number])
        for number, (src, dst) in enumerate(small)
    ]
    for load in small_loads:
        load.start()

    def block(owner_wide, part):
        start = pl.multiple_of(part * half + owner_wide * rows, rows)
        return prem_all.at[pl.ds(start, rows), :]

    def source(a, b):
        return ((hi + n_hi - a) % n_hi) * n_lo + (lo + n_lo - b) % n_lo

    def hi_copy(a, owner):
        return pltpu.make_async_remote_copy(
            src_ref=block(owner, 0),
            dst_ref=block(owner, 0),
            send_sem=ag_send.at[a * n_lo],
            recv_sem=ag_recv.at[a * n_lo],
            device_id=at(hi_peer(a), narrow),
            device_id_type=MESH,
        )

    def lo_copy(a, b, owner):
        return pltpu.make_async_remote_copy(
            src_ref=block(owner, 0),
            dst_ref=block(owner, 0),
            send_sem=ag_send.at[a * n_lo + b],
            recv_sem=ag_recv.at[a * n_lo + b],
            device_id=at(lo_peer(b), narrow),
            device_id_type=MESH,
        )

    def forward(a, b, owner):
        return pltpu.make_async_remote_copy(
            src_ref=block(owner, 0),
            dst_ref=block(owner, 1),
            send_sem=fwd_send.at[a * n_lo + b],
            recv_sem=fwd_recv.at[a * n_lo + b],
            device_id=at(wide, 1 - narrow),
            device_id_type=MESH,
        )

    load_prem.wait()
    prem_all[pl.ds(pl.multiple_of(wide * rows, rows), rows), :] = prem_in[...].astype(jnp.bfloat16)
    pl.semaphore_wait(barrier, n_hi - 1 + n_lo - 1 + 1)
    for b in range(1, n_lo):
        lo_copy(0, b, wide).start()
    for a in near_first:
        hi_copy(a, wide).start()
    forward(0, 0, wide).start()

    load_goals.wait()
    own_rows = pl.ds(pl.multiple_of(narrow * own_goals, own_goals), own_goals)
    goals_all[own_rows, :] = goals_in[...].astype(jnp.bfloat16)
    goal_copy = pltpu.make_async_remote_copy(
        src_ref=goals_all.at[own_rows, :],
        dst_ref=goals_all.at[own_rows, :],
        send_sem=goal_sems.at[0],
        recv_sem=goal_sems.at[1],
        device_id=at(wide, 1 - narrow),
        device_id_type=MESH,
    )
    goal_copy.start()

    all_goals = goals_all.shape[0]
    for load in small_loads:
        load.wait()
    lists = positives_ref[...]
    inverse = 1.0 / counts_ref[...].astype(jnp.float32)
    step = 64

    def weigh(number, carry):
        begin = pl.multiple_of(number * step, step)
        local = begin + lax.broadcasted_iota(jnp.int32, (step, all_goals), 0)
        part = local // half
        inner = local - part * half
        owner = inner // rows
        side = narrow + part * (1 - 2 * narrow)
        ids = (owner * 2 + side) * rows + inner % rows
        total = jnp.zeros((step, all_goals), jnp.float32)
        for slot in range(lists.shape[0]):
            total = total + jnp.where(lists[slot : slot + 1, :] == ids, 1.0, 0.0)
        weights[pl.ds(begin, step), :] = total * inverse
        return carry

    lax.fori_loop(0, 2 * half // step, weigh, 0)

    for a in arrive_first:
        owner = source(a, 0)
        hi_copy(a, owner).wait_recv()
        for b in range(1, n_lo):
            lo_copy(a, b, owner).start()
        forward(a, 0, owner).start()
    for a in [0] + arrive_first:
        for b in range(1, n_lo):
            owner = source(a, b)
            lo_copy(a, b, owner).wait_recv()
            forward(a, b, owner).start()
    goal_copy.wait()

    tall = min(256, half)

    def score(begin):
        span = pl.ds(pl.multiple_of(begin, tall), tall)
        scores[span, :] = (
            lax.dot_general(
                prem_all[span, :],
                goals_all[...],
                (((1,), (1,)), ((), ())),
                preferred_element_type=jnp.float32,
            )
            * scale
        )

    pl.loop(0, half // tall)(lambda number: score(number * tall))
    for a in range(n_hi):
        for b in range(n_lo):
            forward(a, b, source(a, b)).wait_recv()
    pl.loop(0, half // tall)(lambda number: score(half + number * tall))

    lanes = 128

    def soften(number, carry):
        cols = pl.ds(pl.multiple_of(number * lanes, lanes), lanes)
        tile = scores[:, cols]
        weight = weights[:, cols]
        top = jnp.max(tile, axis=0, keepdims=True)
        powers = jnp.exp(tile - top)
        total = jnp.sum(powers, axis=0, keepdims=True)
        positive = jnp.sum(weight * tile, axis=0, keepdims=True)
        loss_ref[:, cols] = top + jnp.log(total) - positive
        factor = cot_ref[:, cols] * scale
        dscores[:, cols] = (factor * (powers * (1.0 / total) - weight)).astype(jnp.bfloat16)
        return carry

    lax.fori_loop(0, all_goals // lanes, soften, 0)

    def premise_gradient(number):
        span = pl.ds(pl.multiple_of(number * tall, tall), tall)
        piece = jnp.dot(dscores[span, :], goals_all[...], preferred_element_type=jnp.float32)
        dprem[span, :] = piece
        lo_out[span, :] = piece.astype(jnp.bfloat16)

    pl.loop(0, half // tall)(premise_gradient)

    def lo_reduce(a, b):
        target_hi = (hi + a) % n_hi
        target = target_hi * n_lo + (lo + b) % n_lo
        return pltpu.make_async_remote_copy(
            src_ref=lo_out.at[pl.ds(pl.multiple_of(target * rows, rows), rows), :],
            dst_ref=lo_in.at[a * n_lo + b],
            send_sem=lo_send.at[a * n_lo + b],
            recv_sem=lo_recv.at[a * n_lo + b],
            device_id=at(lo_peer(b), narrow),
            device_id_type=MESH,
        )

    def hi_reduce(a):
        return pltpu.make_async_remote_copy(
            src_ref=hi_out.at[a],
            dst_ref=hi_in.at[a],
            send_sem=hi_send.at[a],
            recv_sem=hi_recv.at[a],
            device_id=at(hi_peer(a), narrow),
            device_id_type=MESH,
        )

    for a in far_first + [0]:
        for b in range(1, n_lo):
            lo_reduce(a, b).start()

    def pair_sum(a):
        target = hi_peer(a)
        total = dprem[pl.ds(pl.multiple_of(target * rows, rows), rows), :]
        for b in range(1, n_lo):
            lo_reduce(a, b).wait_recv()
            total = total + lo_in[a * n_lo + b].astype(jnp.float32)
        return total

    if n_lo == 1:
        for a in range(1, n_hi):
            hi_out[a] = pair_sum(a).astype(jnp.bfloat16)
            hi_reduce(a).start()

    dgoal[...] = lax.dot_general(
        dscores[:, pl.ds(pl.multiple_of(narrow * own_goals, own_goals), own_goals)],
        prem_all[...],
        (((0,), (0,)), ((), ())),
        preferred_element_type=jnp.float32,
    )

    if n_lo > 1:
        for a in far_first:
            hi_out[a] = pair_sum(a).astype(jnp.bfloat16)
            hi_reduce(a).start()
    mine = pair_sum(0)
    for a in range(1, n_hi):
        hi_reduce(a).wait_recv()
        mine = mine + hi_in[a].astype(jnp.float32)
    dprem_ref[...] = mine

    for a in range(1, n_hi):
        hi_copy(a, wide).wait_send()
        hi_reduce(a).wait_send()
    for a in range(n_hi):
        for b in range(1, n_lo):
            lo_copy(a, b, source(a, 0)).wait_send()
            lo_reduce(a, b).wait_send()
        for b in range(n_lo):
            forward(a, b, source(a, b)).wait_send()


def publish(loss_in, dgoal_in, dprem_in, loss_out, dgoal_out, dprem_out, sems):
    pairs = [(loss_in, loss_out), (dprem_in, dprem_out)]
    pieces = 4
    tall = dgoal_in.shape[0] // pieces
    for number in range(pieces):
        span = pl.ds(number * tall, tall)
        pairs.append((dgoal_in.at[span, :], dgoal_out.at[span, :]))
    copies = [
        pltpu.make_async_copy(src, dst, sems.at[number]) for number, (src, dst) in enumerate(pairs)
    ]
    for copy in copies:
        copy.start()
    for copy in copies:
        copy.wait()


def per_device(n_wide, goals, premises, counts, positives, cotangent):
    n_lo = 2 if n_wide % 2 == 0 else 1
    n_hi = n_wide // n_lo
    own_goals, width = goals.shape
    rows = premises.shape[0]
    all_goals, slots = positives.shape
    half = n_wide * rows
    bf16, f32 = jnp.bfloat16, jnp.float32
    vmem = pl.BlockSpec(memory_space=pltpu.VMEM)
    anywhere = pl.BlockSpec(memory_space=pl.ANY)
    dma = pltpu.SemaphoreType.DMA
    limit = (16 if half <= 512 else 56) * 1024 * 1024
    scratch = [
        pltpu.VMEM((own_goals, width), f32),
        pltpu.VMEM((rows, width), f32),
        pltpu.VMEM((1, all_goals), jnp.int32),
        pltpu.VMEM((slots, all_goals), jnp.int32),
        pltpu.VMEM((1, all_goals), f32),
        pltpu.VMEM((all_goals, width), bf16),
        pltpu.VMEM((2 * half, width), bf16),
        pltpu.VMEM((2 * half, all_goals), f32),
        pltpu.VMEM((2 * half, all_goals), f32),
        pltpu.VMEM((2 * half, all_goals), bf16),
        pltpu.VMEM((half, width), f32),
        pltpu.VMEM((half, width), bf16),
        pltpu.VMEM((n_wide, rows, width), bf16),
        pltpu.VMEM((n_hi, rows, width), bf16),
        pltpu.VMEM((n_hi, rows, width), bf16),
        dma((5,)),
        dma((2,)),
        dma((n_wide,)),
        dma((n_wide,)),
        dma((n_wide,)),
        dma((n_wide,)),
        dma((n_wide,)),
        dma((n_wide,)),
        dma((n_hi,)),
        dma((n_hi,)),
    ]
    found = pl.pallas_call(
        functools.partial(kernel, n_hi, n_lo),
        out_shape=(
            pltpu.VMEM((1, all_goals), f32),
            pltpu.VMEM((own_goals, width), f32),
            pltpu.VMEM((rows, width), f32),
        ),
        in_specs=[pl.BlockSpec(memory_space=pltpu.HBM)] * 5,
        out_specs=(vmem, vmem, vmem),
        scratch_shapes=scratch,
        compiler_params=pltpu.CompilerParams(
            collective_id=0, has_side_effects=True, vmem_limit_bytes=limit
        ),
    )(
        *[
            pltpu.with_memory_space_constraint(x, pltpu.HBM)
            for x in (
                goals,
                premises,
                counts.reshape(1, all_goals),
                positives.T,
                cotangent.reshape(1, all_goals),
            )
        ]
    )
    loss, dgoal, dprem = pl.pallas_call(
        publish,
        out_shape=(
            jax.ShapeDtypeStruct((1, all_goals), f32),
            jax.ShapeDtypeStruct((own_goals, width), f32),
            jax.ShapeDtypeStruct((rows, width), f32),
        ),
        in_specs=[vmem] * 3,
        out_specs=(anywhere,) * 3,
        scratch_shapes=[dma((6,))],
        compiler_params=pltpu.CompilerParams(has_side_effects=True),
    )(*[pltpu.with_memory_space_constraint(x, pltpu.VMEM) for x in found])
    return (loss.reshape(all_goals), dgoal, dprem)


def solution(mesh):
    return jax.shard_map(
        functools.partial(per_device, mesh.shape["wide"]),
        mesh=mesh,
        in_specs=(
            P(("groups", "wide", "narrow"), None),
            P(("groups", "wide", "narrow"), None),
            P(("groups", "wide")),
            P(("groups", "wide"), None),
            P(("groups", "wide")),
        ),
        out_specs=(
            P(("groups", "wide")),
            P(("groups", "wide", "narrow"), None),
            P(("groups", "wide", "narrow"), None),
        ),
        check_vma=False,
    )
```

```python
import functools

import jax
import jax.numpy as jnp
from jax import lax
from jax.experimental import pallas as pl
from jax.experimental.pallas import tpu as pltpu
from jax.sharding import PartitionSpec as P

MESH = pl.DeviceIdType.MESH


def kernel(
    n_hi,
    n_lo,
    cuts,
    goals_hbm,
    prem_hbm,
    counts_hbm,
    positives_hbm,
    cot_hbm,
    loss_ref,
    dgoal,
    dprem_ref,
    goals_in,
    prem_in,
    counts_ref,
    positives_ref,
    cot_ref,
    goals_all,
    prem_all,
    weights,
    scores,
    dscores,
    dprem,
    lo_out,
    lo_in,
    hi_out,
    hi_in,
    local_sems,
    goal_sems,
    ag_send,
    ag_recv,
    fwd_send,
    fwd_recv,
    lo_send,
    lo_recv,
    hi_send,
    hi_recv,
):
    group = lax.axis_index("groups")
    wide = lax.axis_index("wide")
    narrow = lax.axis_index("narrow")
    n_wide = n_hi * n_lo
    hi = wide // n_lo
    lo = wide % n_lo
    rows, width = prem_in.shape
    own_goals = goals_in.shape[0]
    half = n_wide * rows
    short = rows // cuts
    scale = width ** (-0.5)

    def hi_peer(a):
        return ((hi + a) % n_hi) * n_lo + lo

    def lo_peer(b):
        return hi * n_lo + (lo + b) % n_lo

    odd = hi % 2
    if n_hi == 4:
        near_first = [1 + 2 * odd, 3 - 2 * odd, 2]
        arrive_first = [3 - 2 * odd, 1 + 2 * odd, 2]
        first = 3 - 2 * odd
        far_first = [2 + narrow * (first - 2), first + narrow * (2 - first), 1 + 2 * odd]
    else:
        near_first = arrive_first = far_first = list(range(1, n_hi))

    def at(w, n):
        return (group, w, n)

    barrier = pltpu.get_barrier_semaphore()
    for a in range(1, n_hi):
        pl.semaphore_signal(barrier, inc=1, device_id=at(hi_peer(a), narrow), device_id_type=MESH)
    for b in range(1, n_lo):
        pl.semaphore_signal(barrier, inc=1, device_id=at(lo_peer(b), narrow), device_id_type=MESH)
    pl.semaphore_signal(barrier, inc=1, device_id=at(wide, 1 - narrow), device_id_type=MESH)

    load_prem = pltpu.make_async_copy(prem_hbm, prem_in, local_sems.at[0])
    load_prem.start()
    load_goals = pltpu.make_async_copy(goals_hbm, goals_in, local_sems.at[1])
    load_goals.start()
    small = [(counts_hbm, counts_ref), (positives_hbm, positives_ref), (cot_hbm, cot_ref)]
    small_loads = [
        pltpu.make_async_copy(src, dst, local_sems.at[2 + number])
        for number, (src, dst) in enumerate(small)
    ]
    for load in small_loads:
        load.start()

    def block(owner_wide, part, c):
        start = pl.multiple_of(part * half + owner_wide * rows + c * short, short)
        return prem_all.at[pl.ds(start, short), :]

    def source(a, b):
        return ((hi + n_hi - a) % n_hi) * n_lo + (lo + n_lo - b) % n_lo

    def hi_copy(a, owner, c):
        return pltpu.make_async_remote_copy(
            src_ref=block(owner, 0, c),
            dst_ref=block(owner, 0, c),
            send_sem=ag_send.at[a * n_lo * cuts + c],
            recv_sem=ag_recv.at[a * n_lo * cuts + c],
            device_id=at(hi_peer(a), narrow),
            device_id_type=MESH,
        )

    def lo_copy(a, b, owner, c):
        return pltpu.make_async_remote_copy(
            src_ref=block(owner, 0, c),
            dst_ref=block(owner, 0, c),
            send_sem=ag_send.at[(a * n_lo + b) * cuts + c],
            recv_sem=ag_recv.at[(a * n_lo + b) * cuts + c],
            device_id=at(lo_peer(b), narrow),
            device_id_type=MESH,
        )

    def forward(a, b, owner, c):
        return pltpu.make_async_remote_copy(
            src_ref=block(owner, 0, c),
            dst_ref=block(owner, 1, c),
            send_sem=fwd_send.at[(a * n_lo + b) * cuts + c],
            recv_sem=fwd_recv.at[(a * n_lo + b) * cuts + c],
            device_id=at(wide, 1 - narrow),
            device_id_type=MESH,
        )

    load_prem.wait()
    prem_all[pl.ds(pl.multiple_of(wide * rows, rows), rows), :] = prem_in[...].astype(jnp.bfloat16)
    pl.semaphore_wait(barrier, n_hi - 1 + n_lo - 1 + 1)
    for c in range(cuts):
        for b in range(1, n_lo):
            lo_copy(0, b, wide, c).start()
    for a in near_first:
        for c in range(cuts):
            hi_copy(a, wide, c).start()
    for c in range(cuts):
        forward(0, 0, wide, c).start()

    load_goals.wait()
    own_rows = pl.ds(pl.multiple_of(narrow * own_goals, own_goals), own_goals)
    goals_all[own_rows, :] = goals_in[...].astype(jnp.bfloat16)
    goal_copy = pltpu.make_async_remote_copy(
        src_ref=goals_all.at[own_rows, :],
        dst_ref=goals_all.at[own_rows, :],
        send_sem=goal_sems.at[0],
        recv_sem=goal_sems.at[1],
        device_id=at(wide, 1 - narrow),
        device_id_type=MESH,
    )
    goal_copy.start()

    all_goals = goals_all.shape[0]
    for load in small_loads:
        load.wait()
    lists = positives_ref[...]
    inverse = 1.0 / counts_ref[...].astype(jnp.float32)
    step = 64

    def weigh(number, carry):
        begin = pl.multiple_of(number * step, step)
        local = begin + lax.broadcasted_iota(jnp.int32, (step, all_goals), 0)
        part = local // half
        inner = local - part * half
        owner = inner // rows
        side = narrow + part * (1 - 2 * narrow)
        ids = (owner * 2 + side) * rows + inner % rows
        total = jnp.zeros((step, all_goals), jnp.float32)
        for slot in range(lists.shape[0]):
            total = total + jnp.where(lists[slot : slot + 1, :] == ids, 1.0, 0.0)
        weights[pl.ds(begin, step), :] = total * inverse
        return carry

    lax.fori_loop(0, 2 * half // step, weigh, 0)

    for a in arrive_first:
        for c in range(cuts):
            owner = source(a, 0)
            hi_copy(a, owner, c).wait_recv()
            for b in range(1, n_lo):
                lo_copy(a, b, owner, c).start()
            forward(a, 0, owner, c).start()
    for a in [0] + arrive_first:
        for c in range(cuts):
            for b in range(1, n_lo):
                owner = source(a, b)
                lo_copy(a, b, owner, c).wait_recv()
                forward(a, b, owner, c).start()
    goal_copy.wait()

    tall = min(256, half)

    def score(begin):
        span = pl.ds(pl.multiple_of(begin, tall), tall)
        scores[span, :] = (
            lax.dot_general(
                prem_all[span, :],
                goals_all[...],
                (((1,), (1,)), ((), ())),
                preferred_element_type=jnp.float32,
            )
            * scale
        )

    pl.loop(0, half // tall)(lambda number: score(number * tall))
    for a in range(n_hi):
        for b in range(n_lo):
            for c in range(cuts):
                forward(a, b, source(a, b), c).wait_recv()
    pl.loop(0, half // tall)(lambda number: score(half + number * tall))

    lanes = min(256 if half <= 512 else 128, all_goals)

    def soften(number, carry):
        cols = pl.ds(pl.multiple_of(number * lanes, lanes), lanes)
        tile = scores[:, cols]
        weight = weights[:, cols]
        top = jnp.max(tile, axis=0, keepdims=True)
        powers = jnp.exp(tile - top)
        total = jnp.sum(powers, axis=0, keepdims=True)
        positive = jnp.sum(weight * tile, axis=0, keepdims=True)
        loss_ref[:, cols] = top + jnp.log(total) - positive
        factor = cot_ref[:, cols] * scale
        dscores[:, cols] = (factor * (powers * (1.0 / total) - weight)).astype(jnp.bfloat16)
        return carry

    lax.fori_loop(0, all_goals // lanes, soften, 0)

    def premise_gradient(number):
        span = pl.ds(pl.multiple_of(number * tall, tall), tall)
        piece = jnp.dot(dscores[span, :], goals_all[...], preferred_element_type=jnp.float32)
        dprem[span, :] = piece
        lo_out[span, :] = piece.astype(jnp.bfloat16)

    pl.loop(0, half // tall)(premise_gradient)

    def lo_reduce(a, b, c):
        target = (hi + a) % n_hi * n_lo + (lo + b) % n_lo
        start = pl.multiple_of(target * rows + c * short, short)
        return pltpu.make_async_remote_copy(
            src_ref=lo_out.at[pl.ds(start, short), :],
            dst_ref=lo_in.at[a * n_lo + b, pl.ds(c * short, short), :],
            send_sem=lo_send.at[(a * n_lo + b) * cuts + c],
            recv_sem=lo_recv.at[(a * n_lo + b) * cuts + c],
            device_id=at(lo_peer(b), narrow),
            device_id_type=MESH,
        )

    def hi_reduce(a, c):
        return pltpu.make_async_remote_copy(
            src_ref=hi_out.at[a, pl.ds(c * short, short), :],
            dst_ref=hi_in.at[a, pl.ds(c * short, short), :],
            send_sem=hi_send.at[a * cuts + c],
            recv_sem=hi_recv.at[a * cuts + c],
            device_id=at(hi_peer(a), narrow),
            device_id_type=MESH,
        )

    for a in far_first + [0]:
        for c in range(cuts):
            for b in range(1, n_lo):
                lo_reduce(a, b, c).start()

    def pair_sum(a, c):
        start = pl.multiple_of(hi_peer(a) * rows + c * short, short)
        total = dprem[pl.ds(start, short), :]
        for b in range(1, n_lo):
            lo_reduce(a, b, c).wait_recv()
            total = total + lo_in[a * n_lo + b, pl.ds(c * short, short), :].astype(jnp.float32)
        return total

    def send_sums():
        for a in far_first:
            for c in range(cuts):
                hi_out[a, pl.ds(c * short, short), :] = pair_sum(a, c).astype(jnp.bfloat16)
                hi_reduce(a, c).start()

    if n_lo == 1:
        send_sums()
    dgoal[...] = lax.dot_general(
        dscores[:, pl.ds(pl.multiple_of(narrow * own_goals, own_goals), own_goals)],
        prem_all[...],
        (((0,), (0,)), ((), ())),
        preferred_element_type=jnp.float32,
    )

    if n_lo > 1:
        send_sums()
    for c in range(cuts):
        mine = pair_sum(0, c)
        for a in range(1, n_hi):
            hi_reduce(a, c).wait_recv()
            mine = mine + hi_in[a, pl.ds(c * short, short), :].astype(jnp.float32)
        dprem_ref[pl.ds(c * short, short), :] = mine

    for c in range(cuts):
        for a in range(1, n_hi):
            hi_copy(a, wide, c).wait_send()
            hi_reduce(a, c).wait_send()
        for a in range(n_hi):
            for b in range(1, n_lo):
                lo_copy(a, b, source(a, 0), c).wait_send()
                lo_reduce(a, b, c).wait_send()
            for b in range(n_lo):
                forward(a, b, source(a, b), c).wait_send()


def publish(loss_in, dgoal_in, dprem_in, loss_out, dgoal_out, dprem_out, sems):
    pairs = [(loss_in, loss_out), (dprem_in, dprem_out)]
    pieces = 4
    tall = dgoal_in.shape[0] // pieces
    for number in range(pieces):
        span = pl.ds(number * tall, tall)
        pairs.append((dgoal_in.at[span, :], dgoal_out.at[span, :]))
    copies = [
        pltpu.make_async_copy(src, dst, sems.at[number]) for number, (src, dst) in enumerate(pairs)
    ]
    for copy in copies:
        copy.start()
    for copy in copies:
        copy.wait()


def per_device(n_wide, goals, premises, counts, positives, cotangent):
    n_lo = 2 if n_wide % 2 == 0 else 1
    n_hi = n_wide // n_lo
    own_goals, width = goals.shape
    rows = premises.shape[0]
    all_goals, slots = positives.shape
    half = n_wide * rows
    cuts = 2 if rows % 32 == 0 else 1
    bf16, f32 = jnp.bfloat16, jnp.float32
    vmem = pl.BlockSpec(memory_space=pltpu.VMEM)
    anywhere = pl.BlockSpec(memory_space=pl.ANY)
    dma = pltpu.SemaphoreType.DMA
    limit = (16 if half <= 512 else 56) * 1024 * 1024
    scratch = [
        pltpu.VMEM((own_goals, width), f32),
        pltpu.VMEM((rows, width), f32),
        pltpu.VMEM((1, all_goals), jnp.int32),
        pltpu.VMEM((slots, all_goals), jnp.int32),
        pltpu.VMEM((1, all_goals), f32),
        pltpu.VMEM((all_goals, width), bf16),
        pltpu.VMEM((2 * half, width), bf16),
        pltpu.VMEM((2 * half, all_goals), f32),
        pltpu.VMEM((2 * half, all_goals), f32),
        pltpu.VMEM((2 * half, all_goals), bf16),
        pltpu.VMEM((half, width), f32),
        pltpu.VMEM((half, width), bf16),
        pltpu.VMEM((n_wide, rows, width), bf16),
        pltpu.VMEM((n_hi, rows, width), bf16),
        pltpu.VMEM((n_hi, rows, width), bf16),
        dma((5,)),
        dma((2,)),
        dma((n_wide * cuts,)),
        dma((n_wide * cuts,)),
        dma((n_wide * cuts,)),
        dma((n_wide * cuts,)),
        dma((n_wide * cuts,)),
        dma((n_wide * cuts,)),
        dma((n_hi * cuts,)),
        dma((n_hi * cuts,)),
    ]
    found = pl.pallas_call(
        functools.partial(kernel, n_hi, n_lo, cuts),
        out_shape=(
            pltpu.VMEM((1, all_goals), f32),
            pltpu.VMEM((own_goals, width), f32),
            pltpu.VMEM((rows, width), f32),
        ),
        in_specs=[pl.BlockSpec(memory_space=pltpu.HBM)] * 5,
        out_specs=(vmem, vmem, vmem),
        scratch_shapes=scratch,
        compiler_params=pltpu.CompilerParams(
            collective_id=0, has_side_effects=True, vmem_limit_bytes=limit
        ),
    )(
        *[
            pltpu.with_memory_space_constraint(x, pltpu.HBM)
            for x in (
                goals,
                premises,
                counts.reshape(1, all_goals),
                positives.T,
                cotangent.reshape(1, all_goals),
            )
        ]
    )
    loss, dgoal, dprem = pl.pallas_call(
        publish,
        out_shape=(
            jax.ShapeDtypeStruct((1, all_goals), f32),
            jax.ShapeDtypeStruct((own_goals, width), f32),
            jax.ShapeDtypeStruct((rows, width), f32),
        ),
        in_specs=[vmem] * 3,
        out_specs=(anywhere,) * 3,
        scratch_shapes=[dma((6,))],
        compiler_params=pltpu.CompilerParams(has_side_effects=True),
    )(*[pltpu.with_memory_space_constraint(x, pltpu.VMEM) for x in found])
    return (loss.reshape(all_goals), dgoal, dprem)


def solution(mesh):
    return jax.shard_map(
        functools.partial(per_device, mesh.shape["wide"]),
        mesh=mesh,
        in_specs=(
            P(("groups", "wide", "narrow"), None),
            P(("groups", "wide", "narrow"), None),
            P(("groups", "wide")),
            P(("groups", "wide"), None),
            P(("groups", "wide")),
        ),
        out_specs=(
            P(("groups", "wide")),
            P(("groups", "wide", "narrow"), None),
            P(("groups", "wide", "narrow"), None),
        ),
        check_vma=False,
    )
```

```python
import functools

import jax
import jax.numpy as jnp
from jax import lax
from jax.experimental import pallas as pl
from jax.experimental.pallas import tpu as pltpu
from jax.sharding import PartitionSpec as P

MESH = pl.DeviceIdType.MESH


def kernel(
    n_hi,
    n_lo,
    cuts,
    goals_hbm,
    prem_hbm,
    counts_hbm,
    positives_hbm,
    cot_hbm,
    loss_ref,
    dgoal,
    dprem_ref,
    goals_in,
    prem_in,
    counts_ref,
    positives_ref,
    cot_ref,
    goals_all,
    prem_all,
    weights,
    scores,
    dscores,
    dprem,
    lo_out,
    lo_in,
    hi_out,
    hi_in,
    local_sems,
    goal_sems,
    ag_send,
    ag_recv,
    fwd_send,
    fwd_recv,
    lo_send,
    lo_recv,
    hi_send,
    hi_recv,
):
    group = lax.axis_index("groups")
    wide = lax.axis_index("wide")
    narrow = lax.axis_index("narrow")
    n_wide = n_hi * n_lo
    hi = wide // n_lo
    lo = wide % n_lo
    rows, width = prem_in.shape
    own_goals = goals_in.shape[0]
    half = n_wide * rows
    short = rows // cuts
    scale = width ** (-0.5)

    def hi_peer(a):
        return ((hi + a) % n_hi) * n_lo + lo

    def lo_peer(b):
        return hi * n_lo + (lo + b) % n_lo

    odd = hi % 2
    if n_hi == 4:
        cross = 3 - 2 * odd
        near_first = [1 + 2 * odd, cross + narrow * (2 - cross), 2 + narrow * (cross - 2)]
        late = 1 + 2 * odd
        arrive_first = [3 - 2 * odd, late + narrow * (2 - late), 2 + narrow * (late - 2)]
        first = 3 - 2 * odd
        far_first = [2 + narrow * (first - 2), first + narrow * (2 - first), 1 + 2 * odd]
    else:
        near_first = arrive_first = far_first = list(range(1, n_hi))

    def at(w, n):
        return (group, w, n)

    barrier = pltpu.get_barrier_semaphore()
    for a in range(1, n_hi):
        pl.semaphore_signal(barrier, inc=1, device_id=at(hi_peer(a), narrow), device_id_type=MESH)
    for b in range(1, n_lo):
        pl.semaphore_signal(barrier, inc=1, device_id=at(lo_peer(b), narrow), device_id_type=MESH)
    pl.semaphore_signal(barrier, inc=1, device_id=at(wide, 1 - narrow), device_id_type=MESH)

    load_prem = pltpu.make_async_copy(prem_hbm, prem_in, local_sems.at[0])
    load_prem.start()
    load_goals = pltpu.make_async_copy(goals_hbm, goals_in, local_sems.at[1])
    load_goals.start()
    small = [(counts_hbm, counts_ref), (positives_hbm, positives_ref), (cot_hbm, cot_ref)]
    small_loads = [
        pltpu.make_async_copy(src, dst, local_sems.at[2 + number])
        for number, (src, dst) in enumerate(small)
    ]
    for load in small_loads:
        load.start()

    def block(owner_wide, part, c):
        start = pl.multiple_of(part * half + owner_wide * rows + c * short, short)
        return prem_all.at[pl.ds(start, short), :]

    def source(a, b):
        return ((hi + n_hi - a) % n_hi) * n_lo + (lo + n_lo - b) % n_lo

    def hi_copy(a, owner, c):
        return pltpu.make_async_remote_copy(
            src_ref=block(owner, 0, c),
            dst_ref=block(owner, 0, c),
            send_sem=ag_send.at[a * n_lo * cuts + c],
            recv_sem=ag_recv.at[a * n_lo * cuts + c],
            device_id=at(hi_peer(a), narrow),
            device_id_type=MESH,
        )

    def lo_copy(a, b, owner, c):
        return pltpu.make_async_remote_copy(
            src_ref=block(owner, 0, c),
            dst_ref=block(owner, 0, c),
            send_sem=ag_send.at[(a * n_lo + b) * cuts + c],
            recv_sem=ag_recv.at[(a * n_lo + b) * cuts + c],
            device_id=at(lo_peer(b), narrow),
            device_id_type=MESH,
        )

    def forward(a, b, owner, c):
        return pltpu.make_async_remote_copy(
            src_ref=block(owner, 0, c),
            dst_ref=block(owner, 1, c),
            send_sem=fwd_send.at[(a * n_lo + b) * cuts + c],
            recv_sem=fwd_recv.at[(a * n_lo + b) * cuts + c],
            device_id=at(wide, 1 - narrow),
            device_id_type=MESH,
        )

    load_prem.wait()
    prem_all[pl.ds(pl.multiple_of(wide * rows, rows), rows), :] = prem_in[...].astype(jnp.bfloat16)
    pl.semaphore_wait(barrier, n_hi - 1 + n_lo - 1 + 1)
    for c in range(cuts):
        for b in range(1, n_lo):
            lo_copy(0, b, wide, c).start()
    for a in near_first:
        for c in range(cuts):
            hi_copy(a, wide, c).start()
    for c in range(cuts):
        forward(0, 0, wide, c).start()

    load_goals.wait()
    own_rows = pl.ds(pl.multiple_of(narrow * own_goals, own_goals), own_goals)
    goals_all[own_rows, :] = goals_in[...].astype(jnp.bfloat16)
    goal_copy = pltpu.make_async_remote_copy(
        src_ref=goals_all.at[own_rows, :],
        dst_ref=goals_all.at[own_rows, :],
        send_sem=goal_sems.at[0],
        recv_sem=goal_sems.at[1],
        device_id=at(wide, 1 - narrow),
        device_id_type=MESH,
    )
    goal_copy.start()

    all_goals = goals_all.shape[0]
    for load in small_loads:
        load.wait()
    lists = positives_ref[...]
    inverse = 1.0 / counts_ref[...].astype(jnp.float32)
    step = 64

    def weigh(number, carry):
        begin = pl.multiple_of(number * step, step)
        local = begin + lax.broadcasted_iota(jnp.int32, (step, all_goals), 0)
        part = local // half
        inner = local - part * half
        owner = inner // rows
        side = narrow + part * (1 - 2 * narrow)
        ids = (owner * 2 + side) * rows + inner % rows
        total = jnp.zeros((step, all_goals), jnp.float32)
        for slot in range(lists.shape[0]):
            total = total + jnp.where(lists[slot : slot + 1, :] == ids, 1.0, 0.0)
        weights[pl.ds(begin, step), :] = total * inverse
        return carry

    lax.fori_loop(0, 2 * half // step, weigh, 0)

    for a in arrive_first:
        for c in range(cuts):
            owner = source(a, 0)
            hi_copy(a, owner, c).wait_recv()
            for b in range(1, n_lo):
                lo_copy(a, b, owner, c).start()
            forward(a, 0, owner, c).start()
    for a in [0] + arrive_first:
        for c in range(cuts):
            for b in range(1, n_lo):
                owner = source(a, b)
                lo_copy(a, b, owner, c).wait_recv()
                forward(a, b, owner, c).start()
    goal_copy.wait()

    tall = min(256, half)

    def score(begin):
        span = pl.ds(pl.multiple_of(begin, tall), tall)
        scores[span, :] = (
            lax.dot_general(
                prem_all[span, :],
                goals_all[...],
                (((1,), (1,)), ((), ())),
                preferred_element_type=jnp.float32,
            )
            * scale
        )

    pl.loop(0, half // tall)(lambda number: score(number * tall))
    for a in range(n_hi):
        for b in range(n_lo):
            for c in range(cuts):
                forward(a, b, source(a, b), c).wait_recv()
    pl.loop(0, half // tall)(lambda number: score(half + number * tall))

    lanes = min(256 if half <= 512 else 128, all_goals)

    def soften(number, carry):
        cols = pl.ds(pl.multiple_of(number * lanes, lanes), lanes)
        tile = scores[:, cols]
        weight = weights[:, cols]
        top = jnp.max(tile, axis=0, keepdims=True)
        powers = jnp.exp(tile - top)
        total = jnp.sum(powers, axis=0, keepdims=True)
        positive = jnp.sum(weight * tile, axis=0, keepdims=True)
        loss_ref[:, cols] = top + jnp.log(total) - positive
        factor = cot_ref[:, cols] * scale
        dscores[:, cols] = (factor * (powers * (1.0 / total) - weight)).astype(jnp.bfloat16)
        return carry

    lax.fori_loop(0, all_goals // lanes, soften, 0)

    def premise_gradient(number):
        span = pl.ds(pl.multiple_of(number * tall, tall), tall)
        piece = jnp.dot(dscores[span, :], goals_all[...], preferred_element_type=jnp.float32)
        dprem[span, :] = piece
        lo_out[span, :] = piece.astype(jnp.bfloat16)

    pl.loop(0, half // tall)(premise_gradient)

    def lo_reduce(a, b, c):
        target = (hi + a) % n_hi * n_lo + (lo + b) % n_lo
        start = pl.multiple_of(target * rows + c * short, short)
        return pltpu.make_async_remote_copy(
            src_ref=lo_out.at[pl.ds(start, short), :],
            dst_ref=lo_in.at[a * n_lo + b, pl.ds(c * short, short), :],
            send_sem=lo_send.at[(a * n_lo + b) * cuts + c],
            recv_sem=lo_recv.at[(a * n_lo + b) * cuts + c],
            device_id=at(lo_peer(b), narrow),
            device_id_type=MESH,
        )

    def hi_reduce(a, c):
        return pltpu.make_async_remote_copy(
            src_ref=hi_out.at[a, pl.ds(c * short, short), :],
            dst_ref=hi_in.at[a, pl.ds(c * short, short), :],
            send_sem=hi_send.at[a * cuts + c],
            recv_sem=hi_recv.at[a * cuts + c],
            device_id=at(hi_peer(a), narrow),
            device_id_type=MESH,
        )

    for a in far_first + [0]:
        for c in range(cuts):
            for b in range(1, n_lo):
                lo_reduce(a, b, c).start()

    def pair_sum(a, c):
        start = pl.multiple_of(hi_peer(a) * rows + c * short, short)
        total = dprem[pl.ds(start, short), :]
        for b in range(1, n_lo):
            lo_reduce(a, b, c).wait_recv()
            total = total + lo_in[a * n_lo + b, pl.ds(c * short, short), :].astype(jnp.float32)
        return total

    def send_sums():
        for a in far_first:
            for c in range(cuts):
                hi_out[a, pl.ds(c * short, short), :] = pair_sum(a, c).astype(jnp.bfloat16)
                hi_reduce(a, c).start()

    if n_lo == 1:
        send_sums()
    dgoal[...] = lax.dot_general(
        dscores[:, pl.ds(pl.multiple_of(narrow * own_goals, own_goals), own_goals)],
        prem_all[...],
        (((0,), (0,)), ((), ())),
        preferred_element_type=jnp.float32,
    )

    if n_lo > 1:
        send_sums()
    for c in range(cuts):
        mine = pair_sum(0, c)
        for a in range(1, n_hi):
            hi_reduce(a, c).wait_recv()
            mine = mine + hi_in[a, pl.ds(c * short, short), :].astype(jnp.float32)
        dprem_ref[pl.ds(c * short, short), :] = mine

    for c in range(cuts):
        for a in range(1, n_hi):
            hi_copy(a, wide, c).wait_send()
            hi_reduce(a, c).wait_send()
        for a in range(n_hi):
            for b in range(1, n_lo):
                lo_copy(a, b, source(a, 0), c).wait_send()
                lo_reduce(a, b, c).wait_send()
            for b in range(n_lo):
                forward(a, b, source(a, b), c).wait_send()


def publish(loss_in, dgoal_in, dprem_in, loss_out, dgoal_out, dprem_out, sems):
    pairs = [(loss_in, loss_out), (dprem_in, dprem_out)]
    pieces = 1
    tall = dgoal_in.shape[0] // pieces
    for number in range(pieces):
        span = pl.ds(number * tall, tall)
        pairs.append((dgoal_in.at[span, :], dgoal_out.at[span, :]))
    copies = [
        pltpu.make_async_copy(src, dst, sems.at[number]) for number, (src, dst) in enumerate(pairs)
    ]
    for copy in copies:
        copy.start()
    for copy in copies:
        copy.wait()


def per_device(n_wide, goals, premises, counts, positives, cotangent):
    n_lo = 2 if n_wide % 2 == 0 else 1
    n_hi = n_wide // n_lo
    own_goals, width = goals.shape
    rows = premises.shape[0]
    all_goals, slots = positives.shape
    half = n_wide * rows
    cuts = 2 if rows % 32 == 0 else 1
    bf16, f32 = jnp.bfloat16, jnp.float32
    vmem = pl.BlockSpec(memory_space=pltpu.VMEM)
    anywhere = pl.BlockSpec(memory_space=pl.ANY)
    dma = pltpu.SemaphoreType.DMA
    limit = (16 if half <= 512 else 56) * 1024 * 1024
    scratch = [
        pltpu.VMEM((own_goals, width), f32),
        pltpu.VMEM((rows, width), f32),
        pltpu.VMEM((1, all_goals), jnp.int32),
        pltpu.VMEM((slots, all_goals), jnp.int32),
        pltpu.VMEM((1, all_goals), f32),
        pltpu.VMEM((all_goals, width), bf16),
        pltpu.VMEM((2 * half, width), bf16),
        pltpu.VMEM((2 * half, all_goals), f32),
        pltpu.VMEM((2 * half, all_goals), f32),
        pltpu.VMEM((2 * half, all_goals), bf16),
        pltpu.VMEM((half, width), f32),
        pltpu.VMEM((half, width), bf16),
        pltpu.VMEM((n_wide, rows, width), bf16),
        pltpu.VMEM((n_hi, rows, width), bf16),
        pltpu.VMEM((n_hi, rows, width), bf16),
        dma((5,)),
        dma((2,)),
        dma((n_wide * cuts,)),
        dma((n_wide * cuts,)),
        dma((n_wide * cuts,)),
        dma((n_wide * cuts,)),
        dma((n_wide * cuts,)),
        dma((n_wide * cuts,)),
        dma((n_hi * cuts,)),
        dma((n_hi * cuts,)),
    ]
    found = pl.pallas_call(
        functools.partial(kernel, n_hi, n_lo, cuts),
        out_shape=(
            pltpu.VMEM((1, all_goals), f32),
            pltpu.VMEM((own_goals, width), f32),
            pltpu.VMEM((rows, width), f32),
        ),
        in_specs=[pl.BlockSpec(memory_space=pltpu.HBM)] * 5,
        out_specs=(vmem, vmem, vmem),
        scratch_shapes=scratch,
        compiler_params=pltpu.CompilerParams(
            collective_id=0, has_side_effects=True, vmem_limit_bytes=limit
        ),
    )(
        *[
            pltpu.with_memory_space_constraint(x, pltpu.HBM)
            for x in (
                goals,
                premises,
                counts.reshape(1, all_goals),
                positives.T,
                cotangent.reshape(1, all_goals),
            )
        ]
    )
    loss, dgoal, dprem = pl.pallas_call(
        publish,
        out_shape=(
            jax.ShapeDtypeStruct((1, all_goals), f32),
            jax.ShapeDtypeStruct((own_goals, width), f32),
            jax.ShapeDtypeStruct((rows, width), f32),
        ),
        in_specs=[vmem] * 3,
        out_specs=(anywhere,) * 3,
        scratch_shapes=[dma((3,))],
        compiler_params=pltpu.CompilerParams(has_side_effects=True),
    )(*[pltpu.with_memory_space_constraint(x, pltpu.VMEM) for x in found])
    return (loss.reshape(all_goals), dgoal, dprem)


def solution(mesh):
    return jax.shard_map(
        functools.partial(per_device, mesh.shape["wide"]),
        mesh=mesh,
        in_specs=(
            P(("groups", "wide", "narrow"), None),
            P(("groups", "wide", "narrow"), None),
            P(("groups", "wide")),
            P(("groups", "wide"), None),
            P(("groups", "wide")),
        ),
        out_specs=(
            P(("groups", "wide")),
            P(("groups", "wide", "narrow"), None),
            P(("groups", "wide", "narrow"), None),
        ),
        check_vma=False,
    )
```
